32 devices in a mesh: grp: 2 (over y), band: 8 (over z, x), rcv: 2 (over core).
Axes of the slice: x: 2, y: 2, z: 4, core: 2. Of those that a mesh axis runs over, the one named last changes fastest.
Arguments:
- traces: bfloat16 [2048, 1024, 256], P(('grp', 'band'), 'rcv'), parts along dimension 0, may hold values from -6 to 6
Outputs:
- multiples: bfloat16 [2048, 1024, 256], P(('grp', 'band'), 'rcv'), parts along dimension 0
The draws below stay inside these ranges and needn't reach their ends.
There are 2 independent parts, one for each index of `grp`. The reference program is written for one: setup_inputs(seed, part) draws one part's arguments, and reference() takes and returns one part's arrays. A program takes and returns all parts, laid end to end along the dimension named above; each array names one. Nothing has to cross between parts.
All inputs are finite; a program needn't handle non-finite values.
Results may differ from the reference program's by a relative error of at most 0.0082.
Values may be sent and summed in bfloat16 or wider, within the bound.
No kernel may reach another device: no remote copies, remote signals or barrier semaphores. Data moves between devices by JAX's collectives and lax.ppermute only.
A program may use at most 384 MiB of HBM per device.

```python
import math
import jax
import jax.numpy as jnp
from jax import lax

NREC = 1024
NT = 256
N_RCV = 2


def steps_of(stream_key, dims, shards, low, high):
    level, own = 1.0, jax.random.fold_in(stream_key, 6)
    for position, shards_of in shards:
        heights = jnp.exp(jax.random.uniform(jax.random.fold_in(own, position), (shards_of,), jnp.float32, low / len(shards), high / len(shards)))
        level = level * jnp.repeat(heights, dims[position] // shards_of).reshape([-1 if axis == position else 1 for axis in range(len(dims))])
    return level


def noise(stream_key, extent, scale, limit, pieces=(), held_as=jnp.bfloat16):
    gain = steps_of(stream_key, extent, pieces, -0.22, 0.18) if pieces else 1.0
    drawn = jax.random.normal(stream_key, extent, jnp.float32) * scale * gain
    return jnp.minimum(jnp.maximum(drawn, -limit), limit).astype(held_as)


def setup_inputs(seed: int = 0, part: int = 0) -> dict:
    key_list = jax.random.split(jax.random.key(seed), 2)
    part_keys = jax.random.split(jax.random.fold_in(key_list[1], part), 2)
    traces = noise(part_keys[0], (NREC, NREC, NT), 1.0, 6.0, ((0, 8), (1, 2)))
    return dict(traces=traces)


def tables(length):
    times_int = jnp.arange(length, dtype=jnp.int32)
    freqs_int = jnp.arange(length // 2, dtype=jnp.int32)
    phase_int = times_int[:, None] * freqs_int[None, :] % length
    angles = phase_int.astype(jnp.float32) * jnp.float32(2.0 * math.pi / length)
    factor = jnp.float32(1.0 / math.sqrt(length))
    cosine = jnp.cos(angles) * factor
    sine_part = jnp.sin(angles) * factor
    forward = jnp.stack([cosine, -sine_part], axis=2).reshape(length, length).astype(jnp.bfloat16)
    weights = jnp.where(freqs_int == 0, 1.0, 2.0).astype(jnp.float32)
    inverse = jnp.stack([cosine.T * weights[:, None], -sine_part.T * weights[:, None]], axis=1).astype(jnp.bfloat16)
    return (forward, inverse)

def reference(traces):
    forward, inverse = tables(NT)
    spectra = jnp.dot(traces.reshape(NREC * NREC, NT), forward, preferred_element_type=jnp.float32).astype(jnp.bfloat16)
    spectra = spectra.reshape(NREC, NREC, NT // 2, 2).transpose(2, 3, 0, 1)
    width = NREC // N_RCV
    factor = jnp.float32(1.0 / math.sqrt(NREC))
    high = lax.Precision.HIGHEST

    def per_freq(matrix):
        summed = jnp.zeros((2, NREC, NREC), jnp.float32)
        for block_index in range(N_RCV):
            left_part = matrix[:, :, block_index * width:(block_index + 1) * width].astype(jnp.float32)
            right_part = matrix[:, block_index * width:(block_index + 1) * width, :].astype(jnp.float32)
            real_part = jnp.dot(left_part[0], right_part[0], precision=high) - jnp.dot(left_part[1], right_part[1], precision=high)
            imag_part = jnp.dot(left_part[0], right_part[1], precision=high) + jnp.dot(left_part[1], right_part[0], precision=high)
            rounded = (jnp.stack([real_part, imag_part]) * factor).astype(jnp.bfloat16)
            rounded = lax.optimization_barrier(rounded)
            summed = summed + rounded.astype(jnp.float32)
        return summed.astype(jnp.bfloat16)
    multiples_spec = lax.map(per_freq, spectra)
    flat_spec = multiples_spec.reshape(NT, NREC * NREC)
    result = lax.dot_general(flat_spec, inverse.reshape(NT, NT), (((0,), (0,)), ((), ())), preferred_element_type=jnp.float32)
    return result.reshape(NREC, NREC, NT).astype(jnp.bfloat16)
```

```python
import math

import jax
import jax.numpy as jnp
from jax import lax
from jax.experimental import pallas as pl
from jax.experimental.pallas import tpu as pltpu
from jax.sharding import PartitionSpec as P

OWNERS = ("band", "rcv")
SLAB = 16
CHUNKS = 2
LANES = 256
TILE = 128
VMEM = 56 * 2**20


def tables(length):
    times_int = jnp.arange(length, dtype=jnp.int32)
    freqs_int = jnp.arange(length // 2, dtype=jnp.int32)
    phase_int = times_int[:, None] * freqs_int[None, :] % length
    angles = phase_int.astype(jnp.float32) * jnp.float32(2.0 * math.pi / length)
    factor = jnp.float32(1.0 / math.sqrt(length))
    cosine = jnp.cos(angles) * factor
    sine_part = jnp.sin(angles) * factor
    forward = jnp.stack([cosine, -sine_part], axis=2).reshape(length, length).astype(jnp.bfloat16)
    weights = jnp.where(freqs_int == 0, 1.0, 2.0).astype(jnp.float32)
    inverse = jnp.stack(
        [cosine.T * weights[:, None], -sine_part.T * weights[:, None]], axis=1
    ).astype(jnp.bfloat16)
    return (forward, inverse)


def lane_tiles(lanes):
    return [(k, slice(k * TILE, (k + 1) * TILE)) for k in range(lanes // TILE)]


def dft_kernel(traces_ref, table_ref, *refs):
    outs, scratch = refs[:-1], refs[-1]
    sources = traces_ref.shape[0]
    channels = table_ref.shape[0]
    owners, width = outs[0].shape[0], outs[0].shape[1]

    def transform(s, carry):
        spectrum = lax.dot_general(
            table_ref[...], traces_ref[s], (((1,), (1,)), ((), ())), preferred_element_type=jnp.float32
        )
        window = pl.ds(pl.multiple_of(s * channels, channels), channels)
        for k, lanes in lane_tiles(spectrum.shape[1]):
            scratch[k, window, :] = spectrum[:, lanes]
        return carry

    lax.fori_loop(0, sources, transform, 0, unroll=2)

    def regroup(owner, carry):
        for j, out in enumerate(outs):
            for c in range(width):
                row = owner * (width * len(outs)) + j * width + c
                for k, lanes in lane_tiles(out.shape[3]):
                    out[owner, c, :, lanes] = scratch[
                        k, pl.ds(row, sources, stride=channels), :
                    ].astype(jnp.bfloat16)
        return carry

    lax.fori_loop(0, owners, regroup, 0)


def dft(traces, table, first, count, owners, chunks):
    _, receivers, length = traces.shape
    lanes = min(LANES, receivers)
    width = length // (owners * chunks)
    out = jax.ShapeDtypeStruct((owners, width, count * SLAB, receivers), jnp.bfloat16)
    out_spec = pl.BlockSpec((owners, width, SLAB, lanes), lambda i, j: (0, 0, i, j))
    return pl.pallas_call(
        dft_kernel,
        grid=(count, receivers // lanes),
        in_specs=[
            pl.BlockSpec((SLAB, lanes, length), lambda i, j: (i + first, j, 0)),
            pl.BlockSpec((length, length), lambda i, j: (0, 0)),
        ],
        out_specs=[out_spec] * chunks,
        out_shape=[out] * chunks,
        scratch_shapes=[pltpu.VMEM((lanes // TILE, SLAB * length, TILE), jnp.float32)],
        compiler_params=pltpu.CompilerParams(vmem_limit_bytes=VMEM),
        name="dft",
    )(traces, table)


def square_kernel(bands, halves, factor, slab_ref, rest_ref, slab_out, rest_out, real, imag):
    rest = rest_ref.shape[2]
    sources = SLAB + rest
    receivers = rest_ref.shape[3]
    for part, whole in enumerate((real, imag)):
        for b in range(bands):
            for v in range(halves):
                columns = slice(v * receivers, (v + 1) * receivers)
                whole[b * sources : b * sources + SLAB, columns] = slab_ref[b * halves + v, part]
                whole[b * sources + SLAB : (b + 1) * sources, columns] = rest_ref[b * halves + v, part]

    def rows(b, carry):
        window = pl.ds(pl.multiple_of(b * sources, sources), sources)
        left_real, left_imag = real[window, :], imag[window, :]
        for v in range(halves):
            columns = slice(v * receivers, (v + 1) * receivers)
            dot = lambda x, y: jnp.dot(x, y[:, columns], preferred_element_type=jnp.float32)
            out_real = (dot(left_real, real) - dot(left_imag, imag)) * factor
            out_imag = (dot(left_real, imag) + dot(left_imag, real)) * factor
            for part, value in enumerate((out_real, out_imag)):
                value = value.astype(jnp.bfloat16)
                slab_out[b * halves + v, part] = value[:SLAB]
                rest_out[b * halves + v, part] = value[SLAB:]
        return carry

    lax.fori_loop(0, bands, rows, 0)


def square(slab, rest, chunk, bands, halves, factor):
    owners, width, count, receivers = rest.shape
    freqs = width // 2
    stations = bands * (SLAB + count)
    first = chunk * freqs

    def kernel(*refs):
        square_kernel(bands, halves, factor, *refs)

    slab_spec = pl.BlockSpec((owners, 2, SLAB, receivers), lambda f: (0, f, 0, 0))
    rest_spec = pl.BlockSpec((owners, 2, count, receivers), lambda f: (0, f, 0, 0))
    return pl.pallas_call(
        kernel,
        grid=(freqs,),
        in_specs=[
            pl.BlockSpec((owners, 2, SLAB, receivers), lambda f: (0, f + first, 0, 0)),
            rest_spec,
        ],
        out_specs=[slab_spec, rest_spec],
        out_shape=[
            jax.ShapeDtypeStruct((owners, width, SLAB, receivers), jnp.bfloat16),
            jax.ShapeDtypeStruct(rest.shape, jnp.bfloat16),
        ],
        scratch_shapes=[pltpu.VMEM((stations, stations), jnp.bfloat16)] * 2,
        compiler_params=pltpu.CompilerParams(vmem_limit_bytes=VMEM),
        name="square",
    )(slab, rest)


def inverse_kernel(count, *refs):
    spectra, table_ref = refs[:count], refs[count]
    out, scratch = refs[-2], refs[-1]
    owners, width, sources, lanes = spectra[0].shape
    channels = owners * width
    for j, part in enumerate(spectra):

        def widen(owner, carry):
            start = pl.multiple_of((j * owners + owner) * width * sources, width * sources)
            block = part[owner].reshape(width * sources, lanes).astype(jnp.float32)
            for k, window in lane_tiles(lanes):
                scratch[k, pl.ds(start, width * sources), :] = block[:, window]
            return carry

        lax.fori_loop(0, owners, widen, 0)

    def transform(s, carry):
        total = jnp.concatenate(
            [scratch[k, pl.ds(s, count * channels, stride=sources), :] for k, _ in lane_tiles(lanes)],
            axis=1,
        ).astype(jnp.bfloat16)
        out[s] = lax.dot_general(
            total, table_ref[...], (((0,), (0,)), ((), ())), preferred_element_type=jnp.float32
        ).astype(jnp.bfloat16)
        return carry

    lax.fori_loop(0, sources, transform, 0)


def inverse_transform(spectra, table, first, shape, previous):
    owners, width, rows, receivers = spectra[0].shape
    length = shape[2]
    lanes = min(LANES, receivers)
    count = len(spectra)
    spec = pl.BlockSpec((owners, width, SLAB, lanes), lambda i, j: (0, 0, i, j))
    ordered = table.reshape(owners, count, width, length).transpose(1, 0, 2, 3).reshape(length, length)

    def kernel(*refs):
        inverse_kernel(count, *refs)

    in_specs = [spec] * count + [pl.BlockSpec((length, length), lambda i, j: (0, 0))]
    operands = list(spectra) + [ordered]
    aliases = {}
    if previous is not None:
        in_specs.append(pl.BlockSpec(memory_space=pl.ANY))
        operands.append(previous)
        aliases = {count + 1: 0}
    return pl.pallas_call(
        kernel,
        grid=(rows // SLAB, receivers // lanes),
        in_specs=in_specs,
        out_specs=pl.BlockSpec((SLAB, lanes, length), lambda i, j: (i + first, j, 0)),
        out_shape=jax.ShapeDtypeStruct(shape, jnp.bfloat16),
        scratch_shapes=[pltpu.VMEM((lanes // TILE, SLAB * length, TILE), jnp.float32)],
        input_output_aliases=aliases,
        compiler_params=pltpu.CompilerParams(vmem_limit_bytes=VMEM),
        name="inverse",
    )(*operands)


def exchange(array):
    return lax.all_to_all(array, OWNERS, 0, 0)


def body(traces):
    sources, _, length = traces.shape
    bands, halves = lax.axis_size("band"), lax.axis_size("rcv")
    owners = bands * halves
    factor = 1.0 / math.sqrt(sources * bands)
    forward, inverse = tables(length)
    inverse = inverse.reshape(length, length)
    table = forward.T
    slabs = sources // SLAB - 1
    (slab,) = dft(traces, table, 0, 1, owners, 1)
    slab = exchange(slab)
    rest = dft(traces, table, 1, slabs, owners, CHUNKS)
    rest = [exchange(part) for part in rest]
    slab_parts, rest_parts = [], []
    for chunk in range(CHUNKS):
        slab_part, rest_part = square(slab, rest[chunk], chunk, bands, halves, factor)
        slab_parts.append(slab_part)
        rest_parts.append(exchange(rest_part))
    last = exchange(jnp.concatenate(slab_parts, axis=1))
    result = inverse_transform(rest_parts, inverse, 1, traces.shape, None)
    return inverse_transform([last], inverse, 0, traces.shape, result)


def complex_right(rows_part):
    real_part = rows_part[:, 0]
    imag_part = rows_part[:, 1]
    first_row = jnp.stack([real_part, imag_part], axis=1)
    second_row = jnp.stack([-imag_part, real_part], axis=1)
    return jnp.stack([first_row, second_row], axis=1)


def complex_product(left_part, rows_part):
    return jnp.einsum(
        "fqsk,fqpkr->fpsr", left_part, complex_right(rows_part), preferred_element_type=jnp.float32
    )


def general_body(traces):
    length = traces.shape[2]
    stations = traces.shape[0] * lax.axis_size("band")
    factor = jnp.float32(1.0 / math.sqrt(stations))
    forward, inverse = tables(length)
    spectra = jnp.einsum("srt,tc->csr", traces, forward, preferred_element_type=jnp.float32).astype(
        jnp.bfloat16
    )
    owned_spec = lax.all_to_all(spectra, "band", split_axis=0, concat_axis=1, tiled=True)
    channels = owned_spec.shape[0]
    owned_spec = owned_spec.reshape(channels // 2, 2, owned_spec.shape[1], owned_spec.shape[2])
    receiver_panel = lax.all_to_all(owned_spec, "rcv", split_axis=2, concat_axis=3, tiled=True)
    block_terms = complex_product(owned_spec, receiver_panel) * factor
    summed = lax.psum_scatter(
        block_terms.astype(jnp.bfloat16), "rcv", scatter_dimension=3, tiled=True
    )
    source_spec = lax.all_to_all(summed, "band", split_axis=2, concat_axis=0, tiled=True)
    result = jnp.einsum("fpsr,fpt->srt", source_spec, inverse, preferred_element_type=jnp.float32)
    return result.astype(jnp.bfloat16)


def choose(traces):
    sources, _, length = traces.shape
    owners = lax.axis_size("band") * lax.axis_size("rcv")
    if sources % SLAB == 0 and sources > SLAB and (length // 2) % (owners * CHUNKS) == 0:
        return body(traces)
    return general_body(traces)


def solution(mesh):
    placed = (P(("grp", "band"), "rcv", None),)
    return jax.shard_map(
        choose, mesh=mesh, in_specs=placed, out_specs=P(("grp", "band"), "rcv", None), check_vma=False
    )
```

```python
import math

import jax
import jax.numpy as jnp
from jax import lax
from jax.experimental import pallas as pl
from jax.experimental.pallas import tpu as pltpu
from jax.sharding import PartitionSpec as P

OWNERS = ("band", "rcv")
SLAB = 16
CHUNKS = 2
LANES = 256
TILE = 128
PAD = 8
VMEM = 56 * 2**20


def tables(length):
    times_int = jnp.arange(length, dtype=jnp.int32)
    freqs_int = jnp.arange(length // 2, dtype=jnp.int32)
    phase_int = times_int[:, None] * freqs_int[None, :] % length
    angles = phase_int.astype(jnp.float32) * jnp.float32(2.0 * math.pi / length)
    factor = jnp.float32(1.0 / math.sqrt(length))
    cosine = jnp.cos(angles) * factor
    sine_part = jnp.sin(angles) * factor
    forward = jnp.stack([cosine, -sine_part], axis=2).reshape(length, length).astype(jnp.bfloat16)
    weights = jnp.where(freqs_int == 0, 1.0, 2.0).astype(jnp.float32)
    inverse = jnp.stack(
        [cosine.T * weights[:, None], -sine_part.T * weights[:, None]], axis=1
    ).astype(jnp.bfloat16)
    return (forward, inverse)


def lane_tiles(lanes):
    return [(k, slice(k * TILE, (k + 1) * TILE)) for k in range(lanes // TILE)]


def dft_kernel(traces_ref, table_ref, *refs):
    outs, scratch = refs[:-1], refs[-1]
    sources = traces_ref.shape[0]
    channels = table_ref.shape[0]
    owners, width = outs[0].shape[0], outs[0].shape[1]

    def transform(s, carry):
        spectrum = lax.dot_general(
            table_ref[...], traces_ref[s], (((1,), (1,)), ((), ())), preferred_element_type=jnp.float32
        )
        for k, lanes in lane_tiles(spectrum.shape[1]):
            scratch[k, pl.ds(s, channels, stride=sources + PAD), :] = spectrum[:, lanes]
        return carry

    lax.fori_loop(0, sources, transform, 0, unroll=sources)

    def regroup(owner, carry):
        for j, out in enumerate(outs):
            for c in range(width):
                row = (owner * (width * len(outs)) + j * width + c) * (sources + PAD)
                for k, lanes in lane_tiles(out.shape[3]):
                    out[owner, c, :, lanes] = scratch[k, pl.ds(row, sources), :].astype(jnp.bfloat16)
        return carry

    lax.fori_loop(0, owners, regroup, 0, unroll=4)


def dft(traces, table, first, count, owners, chunks):
    _, receivers, length = traces.shape
    lanes = min(LANES, receivers)
    width = length // (owners * chunks)
    out = jax.ShapeDtypeStruct((owners, width, count * SLAB, receivers), jnp.bfloat16)
    out_spec = pl.BlockSpec((owners, width, SLAB, lanes), lambda i, j: (0, 0, i, j))
    return pl.pallas_call(
        dft_kernel,
        grid=(count, receivers // lanes),
        in_specs=[
            pl.BlockSpec((SLAB, lanes, length), lambda i, j: (i + first, j, 0)),
            pl.BlockSpec((length, length), lambda i, j: (0, 0)),
        ],
        out_specs=[out_spec] * chunks,
        out_shape=[out] * chunks,
        scratch_shapes=[pltpu.VMEM((lanes // TILE, length * (SLAB + PAD), TILE), jnp.float32)],
        compiler_params=pltpu.CompilerParams(vmem_limit_bytes=VMEM),
        name="dft",
    )(traces, table)


def square_kernel(bands, halves, factor, slab_ref, rest_ref, slab_out, rest_out, real, imag):
    rest = rest_ref.shape[2]
    sources = SLAB + rest
    receivers = rest_ref.shape[3]
    for part, whole in enumerate((real, imag)):
        for b in range(bands):
            for v in range(halves):
                columns = slice(v * receivers, (v + 1) * receivers)
                whole[b * sources : b * sources + SLAB, columns] = slab_ref[b * halves + v, part]
                whole[b * sources + SLAB : (b + 1) * sources, columns] = rest_ref[b * halves + v, part]

    def rows(b, carry):
        window = pl.ds(pl.multiple_of(b * sources, sources), sources)
        left_real, left_imag = real[window, :], imag[window, :]
        for v in range(halves):
            columns = slice(v * receivers, (v + 1) * receivers)
            dot = lambda x, y: jnp.dot(x, y[:, columns], preferred_element_type=jnp.float32)
            out_real = (dot(left_real, real) - dot(left_imag, imag)) * factor
            out_imag = (dot(left_real, imag) + dot(left_imag, real)) * factor
            for part, value in enumerate((out_real, out_imag)):
                value = value.astype(jnp.bfloat16)
                slab_out[b * halves + v, part] = value[:SLAB]
                rest_out[b * halves + v, part] = value[SLAB:]
        return carry

    lax.fori_loop(0, bands, rows, 0)


def square(slab, rest, chunk, bands, halves, factor):
    owners, width, count, receivers = rest.shape
    freqs = width // 2
    stations = bands * (SLAB + count)
    first = chunk * freqs

    def kernel(*refs):
        square_kernel(bands, halves, factor, *refs)

    slab_spec = pl.BlockSpec((owners, 2, SLAB, receivers), lambda f: (0, f, 0, 0))
    rest_spec = pl.BlockSpec((owners, 2, count, receivers), lambda f: (0, f, 0, 0))
    return pl.pallas_call(
        kernel,
        grid=(freqs,),
        in_specs=[
            pl.BlockSpec((owners, 2, SLAB, receivers), lambda f: (0, f + first, 0, 0)),
            rest_spec,
        ],
        out_specs=[slab_spec, rest_spec],
        out_shape=[
            jax.ShapeDtypeStruct((owners, width, SLAB, receivers), jnp.bfloat16),
            jax.ShapeDtypeStruct(rest.shape, jnp.bfloat16),
        ],
        scratch_shapes=[pltpu.VMEM((stations, stations), jnp.bfloat16)] * 2,
        compiler_params=pltpu.CompilerParams(vmem_limit_bytes=VMEM),
        name="square",
    )(slab, rest)


def inverse_kernel(count, *refs):
    spectra, table_ref = refs[:count], refs[count]
    out, scratch = refs[-2], refs[-1]
    owners, width, sources, lanes = spectra[0].shape
    channels = owners * width
    for j, part in enumerate(spectra):

        def widen(owner, carry):
            for c in range(width):
                row = ((j * owners + owner) * width + c) * (sources + PAD)
                block = part[owner, c].astype(jnp.float32)
                for k, window in lane_tiles(lanes):
                    scratch[k, pl.ds(row, sources), :] = block[:, window]
            return carry

        lax.fori_loop(0, owners, widen, 0, unroll=2)

    def transform(s, carry):
        total = jnp.concatenate(
            [
                scratch[k, pl.ds(s, count * channels, stride=sources + PAD), :]
                for k, _ in lane_tiles(lanes)
            ],
            axis=1,
        ).astype(jnp.bfloat16)
        out[s] = lax.dot_general(
            total, table_ref[...], (((0,), (0,)), ((), ())), preferred_element_type=jnp.float32
        ).astype(jnp.bfloat16)
        return carry

    lax.fori_loop(0, sources, transform, 0, unroll=8)


def inverse_transform(spectra, table, first, shape, previous):
    owners, width, rows, receivers = spectra[0].shape
    length = shape[2]
    lanes = min(LANES, receivers)
    count = len(spectra)
    spec = pl.BlockSpec((owners, width, SLAB, lanes), lambda i, j: (0, 0, i, j))
    ordered = table.reshape(owners, count, width, length).transpose(1, 0, 2, 3).reshape(length, length)

    def kernel(*refs):
        inverse_kernel(count, *refs)

    in_specs = [spec] * count + [pl.BlockSpec((length, length), lambda i, j: (0, 0))]
    operands = list(spectra) + [ordered]
    aliases = {}
    if previous is not None:
        in_specs.append(pl.BlockSpec(memory_space=pl.ANY))
        operands.append(previous)
        aliases = {count + 1: 0}
    return pl.pallas_call(
        kernel,
        grid=(rows // SLAB, receivers // lanes),
        in_specs=in_specs,
        out_specs=pl.BlockSpec((SLAB, lanes, length), lambda i, j: (i + first, j, 0)),
        out_shape=jax.ShapeDtypeStruct(shape, jnp.bfloat16),
        scratch_shapes=[pltpu.VMEM((lanes // TILE, length * (SLAB + PAD), TILE), jnp.float32)],
        input_output_aliases=aliases,
        compiler_params=pltpu.CompilerParams(vmem_limit_bytes=VMEM),
        name="inverse",
    )(*operands)


def exchange(array):
    return lax.all_to_all(array, OWNERS, 0, 0)


def body(traces):
    sources, _, length = traces.shape
    bands, halves = lax.axis_size("band"), lax.axis_size("rcv")
    owners = bands * halves
    factor = 1.0 / math.sqrt(sources * bands)
    forward, inverse = tables(length)
    inverse = inverse.reshape(length, length)
    table = forward.T
    slabs = sources // SLAB - 1
    (slab,) = dft(traces, table, 0, 1, owners, 1)
    slab = exchange(slab)
    rest = dft(traces, table, 1, slabs, owners, CHUNKS)
    rest = [exchange(part) for part in rest]
    slab_parts, rest_parts = [], []
    for chunk in range(CHUNKS):
        slab_part, rest_part = square(slab, rest[chunk], chunk, bands, halves, factor)
        slab_parts.append(slab_part)
        rest_parts.append(exchange(rest_part))
    last = exchange(jnp.concatenate(slab_parts, axis=1))
    result = inverse_transform(rest_parts, inverse, 1, traces.shape, None)
    return inverse_transform([last], inverse, 0, traces.shape, result)


def complex_right(rows_part):
    real_part = rows_part[:, 0]
    imag_part = rows_part[:, 1]
    first_row = jnp.stack([real_part, imag_part], axis=1)
    second_row = jnp.stack([-imag_part, real_part], axis=1)
    return jnp.stack([first_row, second_row], axis=1)


def complex_product(left_part, rows_part):
    return jnp.einsum(
        "fqsk,fqpkr->fpsr", left_part, complex_right(rows_part), preferred_element_type=jnp.float32
    )


def general_body(traces):
    length = traces.shape[2]
    stations = traces.shape[0] * lax.axis_size("band")
    factor = jnp.float32(1.0 / math.sqrt(stations))
    forward, inverse = tables(length)
    spectra = jnp.einsum("srt,tc->csr", traces, forward, preferred_element_type=jnp.float32).astype(
        jnp.bfloat16
    )
    owned_spec = lax.all_to_all(spectra, "band", split_axis=0, concat_axis=1, tiled=True)
    channels = owned_spec.shape[0]
    owned_spec = owned_spec.reshape(channels // 2, 2, owned_spec.shape[1], owned_spec.shape[2])
    receiver_panel = lax.all_to_all(owned_spec, "rcv", split_axis=2, concat_axis=3, tiled=True)
    block_terms = complex_product(owned_spec, receiver_panel) * factor
    summed = lax.psum_scatter(
        block_terms.astype(jnp.bfloat16), "rcv", scatter_dimension=3, tiled=True
    )
    source_spec = lax.all_to_all(summed, "band", split_axis=2, concat_axis=0, tiled=True)
    result = jnp.einsum("fpsr,fpt->srt", source_spec, inverse, preferred_element_type=jnp.float32)
    return result.astype(jnp.bfloat16)


def choose(traces):
    sources, _, length = traces.shape
    owners = lax.axis_size("band") * lax.axis_size("rcv")
    if sources % SLAB == 0 and sources > SLAB and (length // 2) % (owners * CHUNKS) == 0:
        return body(traces)
    return general_body(traces)


def solution(mesh):
    placed = (P(("grp", "band"), "rcv", None),)
    return jax.shard_map(
        choose, mesh=mesh, in_specs=placed, out_specs=P(("grp", "band"), "rcv", None), check_vma=False
    )
```

```python
import math

import jax
import jax.numpy as jnp
import numpy as np
from jax import lax
from jax.experimental import pallas as pl
from jax.experimental.pallas import tpu as pltpu
from jax.sharding import PartitionSpec as P

OWNERS = ("band", "rcv")
SLAB = 8
BLOCK = 24
CHUNKS = 2
LANES = 256
TILE = 128
VMEM = 56 * 2**20


def tables(length):
    times_int = jnp.arange(length, dtype=jnp.int32)
    freqs_int = jnp.arange(length // 2, dtype=jnp.int32)
    phase_int = times_int[:, None] * freqs_int[None, :] % length
    angles = phase_int.astype(jnp.float32) * jnp.float32(2.0 * math.pi / length)
    factor = jnp.float32(1.0 / math.sqrt(length))
    cosine = jnp.cos(angles) * factor
    sine_part = jnp.sin(angles) * factor
    forward = jnp.stack([cosine, -sine_part], axis=2).reshape(length, length).astype(jnp.bfloat16)
    weights = jnp.where(freqs_int == 0, 1.0, 2.0).astype(jnp.float32)
    inverse = jnp.stack(
        [cosine.T * weights[:, None], -sine_part.T * weights[:, None]], axis=1
    ).astype(jnp.bfloat16)
    return (forward, inverse)


def constant_tables(length):
    phase = np.arange(length // 2)[:, None] * np.arange(length)[None, :] % length
    angles = phase.astype(np.float32) * np.float32(2.0 * math.pi / length)
    factor = np.float32(1.0 / math.sqrt(length))
    forward = np.stack([np.cos(angles) * factor, -(np.sin(angles) * factor)], axis=1)
    weights = np.where(np.arange(length // 2) == 0, 1.0, 2.0).astype(np.float32)
    inverse = forward * weights[:, None, None]
    return [array.reshape(length, length).astype(jnp.bfloat16) for array in (forward, inverse)]


def lane_tiles(lanes):
    return [(k, slice(k * TILE, (k + 1) * TILE)) for k in range(lanes // TILE)]


def dft_kernel(traces_ref, table_ref, *refs):
    outs, scratch = refs[:-1], refs[-1]
    sources = traces_ref.shape[0]
    channels = table_ref.shape[0]
    owners, width = outs[0].shape[0], outs[0].shape[1]

    def transform(s, carry):
        spectrum = lax.dot_general(
            table_ref[...], traces_ref[s], (((1,), (1,)), ((), ())), preferred_element_type=jnp.float32
        )
        for k, lanes in lane_tiles(spectrum.shape[1]):
            scratch[k, pl.ds(s, channels, stride=sources), :] = spectrum[:, lanes]
        return carry

    lax.fori_loop(0, sources, transform, 0, unroll=8)

    def regroup(owner, carry):
        for j, out in enumerate(outs):
            for c in range(width):
                row = (owner * (width * len(outs)) + j * width + c) * sources
                for k, lanes in lane_tiles(out.shape[3]):
                    out[owner, c, :, lanes] = scratch[k, pl.ds(row, sources), :].astype(jnp.bfloat16)
        return carry

    lax.fori_loop(0, owners, regroup, 0, unroll=4)


def dft(traces, table, first, count, rows, owners, chunks):
    _, receivers, length = traces.shape
    lanes = min(LANES, receivers)
    width = length // (owners * chunks)
    out = jax.ShapeDtypeStruct((owners, width, count * rows, receivers), jnp.bfloat16)
    out_spec = pl.BlockSpec((owners, width, rows, lanes), lambda i, j: (0, 0, i, j))
    return pl.pallas_call(
        dft_kernel,
        grid=(count, receivers // lanes),
        in_specs=[
            pl.BlockSpec((rows, lanes, length), lambda i, j: (i + first, j, 0)),
            pl.BlockSpec((length, length), lambda i, j: (0, 0)),
        ],
        out_specs=[out_spec] * chunks,
        out_shape=[out] * chunks,
        scratch_shapes=[pltpu.VMEM((lanes // TILE, length * rows, TILE), jnp.float32)],
        compiler_params=pltpu.CompilerParams(vmem_limit_bytes=VMEM),
        name="dft",
    )(traces, table)


def square_kernel(bands, halves, factor, slab_ref, rest_ref, slab_out, rest_out, real, imag):
    rest = rest_ref.shape[2]
    sources = SLAB + rest
    receivers = rest_ref.shape[3]
    for part, whole in enumerate((real, imag)):
        for b in range(bands):
            for v in range(halves):
                columns = slice(v * receivers, (v + 1) * receivers)
                whole[b * sources : b * sources + rest, columns] = rest_ref[b * halves + v, part]
                whole[b * sources + rest : (b + 1) * sources, columns] = slab_ref[b * halves + v, part]

    def rows(b, carry):
        window = pl.ds(pl.multiple_of(b * sources, sources), sources)
        left_real, left_imag = real[window, :], imag[window, :]
        for v in range(halves):
            columns = slice(v * receivers, (v + 1) * receivers)
            dot = lambda x, y: jnp.dot(x, y[:, columns], preferred_element_type=jnp.float32)
            out_real = (dot(left_real, real) - dot(left_imag, imag)) * factor
            out_imag = (dot(left_real, imag) + dot(left_imag, real)) * factor
            for part, value in enumerate((out_real, out_imag)):
                value = value.astype(jnp.bfloat16)
                rest_out[b * halves + v, part] = value[:rest]
                slab_out[b * halves + v, part] = value[rest:]
        return carry

    lax.fori_loop(0, bands, rows, 0)


def square(slab, rest, chunk, bands, halves, factor):
    owners, width, count, receivers = rest.shape
    freqs = width // 2
    stations = bands * (SLAB + count)
    first = chunk * freqs

    def kernel(*refs):
        square_kernel(bands, halves, factor, *refs)

    slab_spec = pl.BlockSpec((owners, 2, SLAB, receivers), lambda f: (0, f, 0, 0))
    rest_spec = pl.BlockSpec((owners, 2, count, receivers), lambda f: (0, f, 0, 0))
    return pl.pallas_call(
        kernel,
        grid=(freqs,),
        in_specs=[
            pl.BlockSpec((owners, 2, SLAB, receivers), lambda f: (0, f + first, 0, 0)),
            rest_spec,
        ],
        out_specs=[slab_spec, rest_spec],
        out_shape=[
            jax.ShapeDtypeStruct((owners, width, SLAB, receivers), jnp.bfloat16),
            jax.ShapeDtypeStruct(rest.shape, jnp.bfloat16),
        ],
        scratch_shapes=[pltpu.VMEM((stations, stations), jnp.bfloat16)] * 2,
        compiler_params=pltpu.CompilerParams(vmem_limit_bytes=VMEM),
        name="square",
    )(slab, rest)


def inverse_kernel(count, *refs):
    spectra, table_ref = refs[:count], refs[count]
    out, scratch = refs[-2], refs[-1]
    owners, width, sources, lanes = spectra[0].shape
    channels = owners * width
    for j, part in enumerate(spectra):

        def widen(owner, carry):
            for c in range(width):
                row = ((j * owners + owner) * width + c) * sources
                block = part[owner, c].astype(jnp.float32)
                for k, window in lane_tiles(lanes):
                    scratch[k, pl.ds(row, sources), :] = block[:, window]
            return carry

        lax.fori_loop(0, owners, widen, 0, unroll=2)

    def transform(s, carry):
        total = jnp.concatenate(
            [
                scratch[k, pl.ds(s, count * channels, stride=sources), :]
                for k, _ in lane_tiles(lanes)
            ],
            axis=1,
        ).astype(jnp.bfloat16)
        out[s] = lax.dot_general(
            total, table_ref[...], (((0,), (0,)), ((), ())), preferred_element_type=jnp.float32
        ).astype(jnp.bfloat16)
        return carry

    lax.fori_loop(0, sources, transform, 0, unroll=8)


def inverse_transform(spectra, table, first, rows, shape, previous):
    owners, width, total, receivers = spectra[0].shape
    length = shape[2]
    lanes = min(LANES, receivers)
    count = len(spectra)
    spec = pl.BlockSpec((owners, width, rows, lanes), lambda i, j: (0, 0, i, j))
    ordered = table.reshape(owners, count, width, length).transpose(1, 0, 2, 3).reshape(length, length)

    def kernel(*refs):
        inverse_kernel(count, *refs)

    in_specs = [spec] * count + [pl.BlockSpec((length, length), lambda i, j: (0, 0))]
    operands = list(spectra) + [ordered]
    aliases = {}
    if previous is not None:
        in_specs.append(pl.BlockSpec(memory_space=pl.ANY))
        operands.append(previous)
        aliases = {count + 1: 0}
    return pl.pallas_call(
        kernel,
        grid=(total // rows, receivers // lanes),
        in_specs=in_specs,
        out_specs=pl.BlockSpec((rows, lanes, length), lambda i, j: (i + first, j, 0)),
        out_shape=jax.ShapeDtypeStruct(shape, jnp.bfloat16),
        scratch_shapes=[pltpu.VMEM((lanes // TILE, length * rows, TILE), jnp.float32)],
        input_output_aliases=aliases,
        compiler_params=pltpu.CompilerParams(vmem_limit_bytes=VMEM),
        name="inverse",
    )(*operands)


def exchange(array):
    return lax.all_to_all(array, OWNERS, 0, 0)


def body(traces):
    sources, _, length = traces.shape
    bands, halves = lax.axis_size("band"), lax.axis_size("rcv")
    owners = bands * halves
    factor = 1.0 / math.sqrt(sources * bands)
    table, inverse = constant_tables(length)
    rest_count = sources - SLAB
    (slab,) = dft(traces, table, rest_count // SLAB, 1, SLAB, owners, 1)
    slab = exchange(slab)
    rest = dft(traces, table, 0, rest_count // BLOCK, BLOCK, owners, CHUNKS)
    rest = [exchange(part) for part in rest]
    slab_parts, rest_parts = [], []
    for chunk in range(CHUNKS):
        slab_part, rest_part = square(slab, rest[chunk], chunk, bands, halves, factor)
        slab_parts.append(slab_part)
        rest_parts.append(exchange(rest_part))
    last = exchange(jnp.concatenate(slab_parts, axis=1))
    result = inverse_transform(rest_parts, inverse, 0, BLOCK, traces.shape, None)
    return inverse_transform([last], inverse, rest_count // SLAB, SLAB, traces.shape, result)


def complex_right(rows_part):
    real_part = rows_part[:, 0]
    imag_part = rows_part[:, 1]
    first_row = jnp.stack([real_part, imag_part], axis=1)
    second_row = jnp.stack([-imag_part, real_part], axis=1)
    return jnp.stack([first_row, second_row], axis=1)


def complex_product(left_part, rows_part):
    return jnp.einsum(
        "fqsk,fqpkr->fpsr", left_part, complex_right(rows_part), preferred_element_type=jnp.float32
    )


def general_body(traces):
    length = traces.shape[2]
    stations = traces.shape[0] * lax.axis_size("band")
    factor = jnp.float32(1.0 / math.sqrt(stations))
    forward, inverse = tables(length)
    spectra = jnp.einsum("srt,tc->csr", traces, forward, preferred_element_type=jnp.float32).astype(
        jnp.bfloat16
    )
    owned_spec = lax.all_to_all(spectra, "band", split_axis=0, concat_axis=1, tiled=True)
    channels = owned_spec.shape[0]
    owned_spec = owned_spec.reshape(channels // 2, 2, owned_spec.shape[1], owned_spec.shape[2])
    receiver_panel = lax.all_to_all(owned_spec, "rcv", split_axis=2, concat_axis=3, tiled=True)
    block_terms = complex_product(owned_spec, receiver_panel) * factor
    summed = lax.psum_scatter(
        block_terms.astype(jnp.bfloat16), "rcv", scatter_dimension=3, tiled=True
    )
    source_spec = lax.all_to_all(summed, "band", split_axis=2, concat_axis=0, tiled=True)
    result = jnp.einsum("fpsr,fpt->srt", source_spec, inverse, preferred_element_type=jnp.float32)
    return result.astype(jnp.bfloat16)


def choose(traces):
    sources, _, length = traces.shape
    owners = lax.axis_size("band") * lax.axis_size("rcv")
    rest = sources - SLAB
    fits = sources % SLAB == 0 and rest > 0 and rest % BLOCK == 0
    if fits and (length // 2) % (owners * CHUNKS) == 0:
        return body(traces)
    return general_body(traces)


def solution(mesh):
    placed = (P(("grp", "band"), "rcv", None),)
    return jax.shard_map(
        choose, mesh=mesh, in_specs=placed, out_specs=P(("grp", "band"), "rcv", None), check_vma=False
    )
```

```python
import math

import jax
import jax.numpy as jnp
import numpy as np
from jax import lax
from jax.experimental import pallas as pl
from jax.experimental.pallas import tpu as pltpu
from jax.sharding import PartitionSpec as P

OWNERS = ("band", "rcv")
SLAB = 8
BLOCK = 24
CHUNKS = 2
LANES = 256
TILE = 128
VMEM = 62 * 2**20


def tables(length):
    times_int = jnp.arange(length, dtype=jnp.int32)
    freqs_int = jnp.arange(length // 2, dtype=jnp.int32)
    phase_int = times_int[:, None] * freqs_int[None, :] % length
    angles = phase_int.astype(jnp.float32) * jnp.float32(2.0 * math.pi / length)
    factor = jnp.float32(1.0 / math.sqrt(length))
    cosine = jnp.cos(angles) * factor
    sine_part = jnp.sin(angles) * factor
    forward = jnp.stack([cosine, -sine_part], axis=2).reshape(length, length).astype(jnp.bfloat16)
    weights = jnp.where(freqs_int == 0, 1.0, 2.0).astype(jnp.float32)
    inverse = jnp.stack(
        [cosine.T * weights[:, None], -sine_part.T * weights[:, None]], axis=1
    ).astype(jnp.bfloat16)
    return (forward, inverse)


def constant_tables(length):
    phase = np.arange(length // 2)[:, None] * np.arange(length)[None, :] % length
    angles = phase.astype(np.float32) * np.float32(2.0 * math.pi / length)
    factor = np.float32(1.0 / math.sqrt(length))
    forward = np.stack([np.cos(angles) * factor, -(np.sin(angles) * factor)], axis=1)
    weights = np.where(np.arange(length // 2) == 0, 1.0, 2.0).astype(np.float32)
    inverse = forward * weights[:, None, None]
    return [array.reshape(length, length).astype(jnp.bfloat16) for array in (forward, inverse)]


def lane_tiles(lanes):
    return [(k, slice(k * TILE, (k + 1) * TILE)) for k in range(lanes // TILE)]


def dft_kernel(traces_ref, table_ref, *refs):
    outs, scratch = refs[:-1], refs[-1]
    sources = traces_ref.shape[0]
    channels = table_ref.shape[0]
    owners, width = outs[0].shape[0], outs[0].shape[1]

    def transform(s, carry):
        spectrum = lax.dot_general(
            table_ref[...], traces_ref[s], (((1,), (1,)), ((), ())), preferred_element_type=jnp.float32
        )
        for k, lanes in lane_tiles(spectrum.shape[1]):
            scratch[k, pl.ds(s, channels, stride=sources), :] = spectrum[:, lanes]
        return carry

    lax.fori_loop(0, sources, transform, 0, unroll=8)

    def regroup(owner, carry):
        for j, out in enumerate(outs):
            for c in range(width):
                row = (owner * (width * len(outs)) + j * width + c) * sources
                for k, lanes in lane_tiles(out.shape[3]):
                    out[owner, c, :, lanes] = scratch[k, pl.ds(row, sources), :].astype(jnp.bfloat16)
        return carry

    lax.fori_loop(0, owners, regroup, 0, unroll=4)


def dft(traces, table, first, count, rows, owners, chunks):
    _, receivers, length = traces.shape
    lanes = min(LANES, receivers)
    width = length // (owners * chunks)
    out = jax.ShapeDtypeStruct((owners, width, count * rows, receivers), jnp.bfloat16)
    out_spec = pl.BlockSpec((owners, width, rows, lanes), lambda i, j: (0, 0, i, j))
    return pl.pallas_call(
        dft_kernel,
        grid=(count, receivers // lanes),
        in_specs=[
            pl.BlockSpec((rows, lanes, length), lambda i, j: (i + first, j, 0)),
            pl.BlockSpec((length, length), lambda i, j: (0, 0)),
        ],
        out_specs=[out_spec] * chunks,
        out_shape=[out] * chunks,
        scratch_shapes=[pltpu.VMEM((lanes // TILE, length * rows, TILE), jnp.float32)],
        compiler_params=pltpu.CompilerParams(vmem_limit_bytes=VMEM),
        name="dft",
    )(traces, table)


def square_kernel(bands, halves, factor, slab_ref, rest_ref, slab_out, rest_out, real, imag):
    rest = rest_ref.shape[2]
    sources = SLAB + rest
    receivers = rest_ref.shape[3]
    for part, whole in enumerate((real, imag)):
        for b in range(bands):
            for v in range(halves):
                columns = slice(v * receivers, (v + 1) * receivers)
                whole[b * sources : b * sources + rest, columns] = rest_ref[b * halves + v, part]
                whole[b * sources + rest : (b + 1) * sources, columns] = slab_ref[b * halves + v, part]

    def rows(b, carry):
        window = pl.ds(pl.multiple_of(b * sources, sources), sources)
        left_real, left_imag = real[window, :], imag[window, :]
        for v in range(halves):
            columns = slice(v * receivers, (v + 1) * receivers)
            dot = lambda x, y: jnp.dot(x, y[:, columns], preferred_element_type=jnp.float32)
            out_real = (dot(left_real, real) - dot(left_imag, imag)) * factor
            out_imag = (dot(left_real, imag) + dot(left_imag, real)) * factor
            for part, value in enumerate((out_real, out_imag)):
                value = value.astype(jnp.bfloat16)
                rest_out[b * halves + v, part] = value[:rest]
                slab_out[b * halves + v, part] = value[rest:]
        return carry

    lax.fori_loop(0, bands, rows, 0)


def square(slab, rest, chunk, bands, halves, factor):
    owners, width, count, receivers = rest.shape
    freqs = width // 2
    stations = bands * (SLAB + count)
    first = chunk * freqs

    def kernel(*refs):
        square_kernel(bands, halves, factor, *refs)

    slab_spec = pl.BlockSpec((owners, 2, SLAB, receivers), lambda f: (0, f, 0, 0))
    rest_spec = pl.BlockSpec((owners, 2, count, receivers), lambda f: (0, f, 0, 0))
    return pl.pallas_call(
        kernel,
        grid=(freqs,),
        in_specs=[
            pl.BlockSpec((owners, 2, SLAB, receivers), lambda f: (0, f + first, 0, 0)),
            rest_spec,
        ],
        out_specs=[slab_spec, rest_spec],
        out_shape=[
            jax.ShapeDtypeStruct((owners, width, SLAB, receivers), jnp.bfloat16),
            jax.ShapeDtypeStruct(rest.shape, jnp.bfloat16),
        ],
        scratch_shapes=[pltpu.VMEM((stations, stations), jnp.bfloat16)] * 2,
        compiler_params=pltpu.CompilerParams(vmem_limit_bytes=VMEM),
        name="square",
    )(slab, rest)


def inverse_kernel(count, *refs):
    spectra, table_ref = refs[:count], refs[count]
    out, scratch = refs[-2], refs[-1]
    owners, width, sources, lanes = spectra[0].shape
    channels = owners * width
    for j, part in enumerate(spectra):

        def widen(owner, carry):
            for c in range(width):
                row = ((j * owners + owner) * width + c) * sources
                block = part[owner, c].astype(jnp.float32)
                for k, window in lane_tiles(lanes):
                    scratch[k, pl.ds(row, sources), :] = block[:, window]
            return carry

        lax.fori_loop(0, owners, widen, 0, unroll=2)

    def transform(s, carry):
        total = jnp.concatenate(
            [
                scratch[k, pl.ds(s, count * channels, stride=sources), :]
                for k, _ in lane_tiles(lanes)
            ],
            axis=1,
        ).astype(jnp.bfloat16)
        out[s] = lax.dot_general(
            total, table_ref[...], (((0,), (0,)), ((), ())), preferred_element_type=jnp.float32
        ).astype(jnp.bfloat16)
        return carry

    lax.fori_loop(0, sources, transform, 0, unroll=8)


def inverse_transform(spectra, table, first, rows, shape, previous):
    owners, width, total, receivers = spectra[0].shape
    length = shape[2]
    lanes = min(LANES, receivers)
    count = len(spectra)
    spec = pl.BlockSpec((owners, width, rows, lanes), lambda i, j: (0, 0, i, j))
    ordered = table.reshape(owners, count, width, length).transpose(1, 0, 2, 3).reshape(length, length)

    def kernel(*refs):
        inverse_kernel(count, *refs)

    in_specs = [spec] * count + [pl.BlockSpec((length, length), lambda i, j: (0, 0))]
    operands = list(spectra) + [ordered]
    aliases = {}
    if previous is not None:
        in_specs.append(pl.BlockSpec(memory_space=pl.ANY))
        operands.append(previous)
        aliases = {count + 1: 0}
    return pl.pallas_call(
        kernel,
        grid=(total // rows, receivers // lanes),
        in_specs=in_specs,
        out_specs=pl.BlockSpec((rows, lanes, length), lambda i, j: (i + first, j, 0)),
        out_shape=jax.ShapeDtypeStruct(shape, jnp.bfloat16),
        scratch_shapes=[pltpu.VMEM((lanes // TILE, length * rows, TILE), jnp.float32)],
        input_output_aliases=aliases,
        compiler_params=pltpu.CompilerParams(vmem_limit_bytes=VMEM),
        name="inverse",
    )(*operands)


def exchange(array):
    return lax.all_to_all(array, OWNERS, 0, 0)


def body(traces):
    sources, _, length = traces.shape
    bands, halves = lax.axis_size("band"), lax.axis_size("rcv")
    owners = bands * halves
    factor = 1.0 / math.sqrt(sources * bands)
    table, inverse = constant_tables(length)
    rest_count = sources - SLAB
    (slab,) = dft(traces, table, rest_count // SLAB, 1, SLAB, owners, 1)
    slab = exchange(slab)
    rest = dft(traces, table, 0, rest_count // BLOCK, BLOCK, owners, CHUNKS)
    rest = [exchange(part) for part in rest]
    slab_parts, rest_parts = [], []
    for chunk in range(CHUNKS):
        slab_part, rest_part = square(slab, rest[chunk], chunk, bands, halves, factor)
        slab_parts.append(slab_part)
        rest_parts.append(exchange(rest_part))
    last = exchange(jnp.concatenate(slab_parts, axis=1))
    result = inverse_transform(rest_parts, inverse, 0, BLOCK, traces.shape, None)
    return inverse_transform([last], inverse, rest_count // SLAB, SLAB, traces.shape, result)


def complex_right(rows_part):
    real_part = rows_part[:, 0]
    imag_part = rows_part[:, 1]
    first_row = jnp.stack([real_part, imag_part], axis=1)
    second_row = jnp.stack([-imag_part, real_part], axis=1)
    return jnp.stack([first_row, second_row], axis=1)


def complex_product(left_part, rows_part):
    return jnp.einsum(
        "fqsk,fqpkr->fpsr", left_part, complex_right(rows_part), preferred_element_type=jnp.float32
    )


def general_body(traces):
    length = traces.shape[2]
    stations = traces.shape[0] * lax.axis_size("band")
    factor = jnp.float32(1.0 / math.sqrt(stations))
    forward, inverse = tables(length)
    spectra = jnp.einsum("srt,tc->csr", traces, forward, preferred_element_type=jnp.float32).astype(
        jnp.bfloat16
    )
    owned_spec = lax.all_to_all(spectra, "band", split_axis=0, concat_axis=1, tiled=True)
    channels = owned_spec.shape[0]
    owned_spec = owned_spec.reshape(channels // 2, 2, owned_spec.shape[1], owned_spec.shape[2])
    receiver_panel = lax.all_to_all(owned_spec, "rcv", split_axis=2, concat_axis=3, tiled=True)
    block_terms = complex_product(owned_spec, receiver_panel) * factor
    summed = lax.psum_scatter(
        block_terms.astype(jnp.bfloat16), "rcv", scatter_dimension=3, tiled=True
    )
    source_spec = lax.all_to_all(summed, "band", split_axis=2, concat_axis=0, tiled=True)
    result = jnp.einsum("fpsr,fpt->srt", source_spec, inverse, preferred_element_type=jnp.float32)
    return result.astype(jnp.bfloat16)


def choose(traces):
    sources, _, length = traces.shape
    owners = lax.axis_size("band") * lax.axis_size("rcv")
    rest = sources - SLAB
    fits = sources % SLAB == 0 and rest > 0 and rest % BLOCK == 0
    if fits and (length // 2) % (owners * CHUNKS) == 0:
        return body(traces)
    return general_body(traces)


def solution(mesh):
    placed = (P(("grp", "band"), "rcv", None),)
    return jax.shard_map(
        choose, mesh=mesh, in_specs=placed, out_specs=P(("grp", "band"), "rcv", None), check_vma=False
    )
```

```python
import math

import jax
import jax.numpy as jnp
import numpy as np
from jax import lax
from jax.experimental import pallas as pl
from jax.experimental.pallas import tpu as pltpu
from jax.sharding import PartitionSpec as P

OWNERS = ("band", "rcv")
SLAB = 8
BLOCK = 24
CHUNKS = 2
LANES = 256
TILE = 128
VMEM = 62 * 2**20


def tables(length):
    times_int = jnp.arange(length, dtype=jnp.int32)
    freqs_int = jnp.arange(length // 2, dtype=jnp.int32)
    phase_int = times_int[:, None] * freqs_int[None, :] % length
    angles = phase_int.astype(jnp.float32) * jnp.float32(2.0 * math.pi / length)
    factor = jnp.float32(1.0 / math.sqrt(length))
    cosine = jnp.cos(angles) * factor
    sine_part = jnp.sin(angles) * factor
    forward = jnp.stack([cosine, -sine_part], axis=2).reshape(length, length).astype(jnp.bfloat16)
    weights = jnp.where(freqs_int == 0, 1.0, 2.0).astype(jnp.float32)
    inverse = jnp.stack(
        [cosine.T * weights[:, None], -sine_part.T * weights[:, None]], axis=1
    ).astype(jnp.bfloat16)
    return (forward, inverse)


def constant_tables(length):
    phase = np.arange(length // 2)[:, None] * np.arange(length)[None, :] % length
    angles = phase.astype(np.float32) * np.float32(2.0 * math.pi / length)
    factor = np.float32(1.0 / math.sqrt(length))
    forward = np.stack([np.cos(angles) * factor, -(np.sin(angles) * factor)], axis=1)
    weights = np.where(np.arange(length // 2) == 0, 1.0, 2.0).astype(np.float32)
    inverse = forward * weights[:, None, None]
    return [array.reshape(length, length).astype(jnp.bfloat16) for array in (forward, inverse)]


def lane_tiles(lanes):
    return [(k, slice(k * TILE, (k + 1) * TILE)) for k in range(lanes // TILE)]


def dft_kernel(traces_ref, table_ref, *refs):
    outs, scratch = refs[:-1], refs[-1]
    sources = traces_ref.shape[0]
    channels = table_ref.shape[0]
    owners, width = outs[0].shape[0], outs[0].shape[1]

    def transform(s, carry):
        spectrum = lax.dot_general(
            table_ref[...], traces_ref[s], (((1,), (1,)), ((), ())), preferred_element_type=jnp.float32
        )
        for k, lanes in lane_tiles(spectrum.shape[1]):
            scratch[k, pl.ds(s, channels, stride=sources), :] = spectrum[:, lanes]
        return carry

    lax.fori_loop(0, sources, transform, 0, unroll=8)

    def regroup(owner, carry):
        for j, out in enumerate(outs):
            for c in range(width):
                row = (owner * (width * len(outs)) + j * width + c) * sources
                for k, lanes in lane_tiles(out.shape[3]):
                    out[owner, c, :, lanes] = scratch[k, pl.ds(row, sources), :].astype(jnp.bfloat16)
        return carry

    lax.fori_loop(0, owners, regroup, 0, unroll=4)


def dft(traces, table, first, count, rows, owners, chunks):
    _, receivers, length = traces.shape
    lanes = min(LANES, receivers)
    channels = table.shape[0]
    width = channels // (owners * chunks)
    out = jax.ShapeDtypeStruct((owners, width, count * rows, receivers), jnp.bfloat16)
    out_spec = pl.BlockSpec((owners, width, rows, lanes), lambda i, j: (0, 0, i, j))
    return pl.pallas_call(
        dft_kernel,
        grid=(count, receivers // lanes),
        in_specs=[
            pl.BlockSpec((rows, lanes, length), lambda i, j: (i + first, j, 0)),
            pl.BlockSpec((channels, length), lambda i, j: (0, 0)),
        ],
        out_specs=[out_spec] * chunks,
        out_shape=[out] * chunks,
        scratch_shapes=[pltpu.VMEM((lanes // TILE, channels * rows, TILE), jnp.float32)],
        compiler_params=pltpu.CompilerParams(vmem_limit_bytes=VMEM),
        name="dft",
    )(traces, table)


def square_kernel(bands, halves, factor, slab_ref, rest_ref, slab_out, rest_out, real, imag):
    rest = rest_ref.shape[2]
    sources = SLAB + rest
    receivers = rest_ref.shape[3]
    for part, whole in enumerate((real, imag)):
        for b in range(bands):
            for v in range(halves):
                columns = slice(v * receivers, (v + 1) * receivers)
                whole[b * sources : b * sources + rest, columns] = rest_ref[b * halves + v, part]
                whole[b * sources + rest : (b + 1) * sources, columns] = slab_ref[b * halves + v, part]

    def rows(b, carry):
        window = pl.ds(pl.multiple_of(b * sources, sources), sources)
        left_real, left_imag = real[window, :], imag[window, :]
        for v in range(halves):
            columns = slice(v * receivers, (v + 1) * receivers)
            dot = lambda x, y: jnp.dot(x, y[:, columns], preferred_element_type=jnp.float32)
            out_real = (dot(left_real, real) - dot(left_imag, imag)) * factor
            out_imag = (dot(left_real, imag) + dot(left_imag, real)) * factor
            for part, value in enumerate((out_real, out_imag)):
                value = value.astype(jnp.bfloat16)
                rest_out[b * halves + v, part] = value[:rest]
                slab_out[b * halves + v, part] = value[rest:]
        return carry

    lax.fori_loop(0, bands, rows, 0)


def square(slab, rest, chunk, bands, halves, factor):
    owners, width, count, receivers = rest.shape
    freqs = width // 2
    stations = bands * (SLAB + count)
    first = chunk * freqs

    def kernel(*refs):
        square_kernel(bands, halves, factor, *refs)

    slab_spec = pl.BlockSpec((owners, 2, SLAB, receivers), lambda f: (0, f, 0, 0))
    rest_spec = pl.BlockSpec((owners, 2, count, receivers), lambda f: (0, f, 0, 0))
    return pl.pallas_call(
        kernel,
        grid=(freqs,),
        in_specs=[
            pl.BlockSpec((owners, 2, SLAB, receivers), lambda f: (0, f + first, 0, 0)),
            rest_spec,
        ],
        out_specs=[slab_spec, rest_spec],
        out_shape=[
            jax.ShapeDtypeStruct((owners, width, SLAB, receivers), jnp.bfloat16),
            jax.ShapeDtypeStruct(rest.shape, jnp.bfloat16),
        ],
        scratch_shapes=[pltpu.VMEM((stations, stations), jnp.bfloat16)] * 2,
        compiler_params=pltpu.CompilerParams(vmem_limit_bytes=VMEM),
        name="square",
    )(slab, rest)


def inverse_kernel(count, *refs):
    spectra, table_ref = refs[:count], refs[count]
    out, scratch = refs[-2], refs[-1]
    owners, width, sources, lanes = spectra[0].shape
    channels = owners * width
    for j, part in enumerate(spectra):

        def widen(owner, carry):
            for c in range(width):
                row = ((j * owners + owner) * width + c) * sources
                block = part[owner, c].astype(jnp.float32)
                for k, window in lane_tiles(lanes):
                    scratch[k, pl.ds(row, sources), :] = block[:, window]
            return carry

        lax.fori_loop(0, owners, widen, 0, unroll=2)

    def transform(s, carry):
        total = jnp.concatenate(
            [
                scratch[k, pl.ds(s, count * channels, stride=sources), :]
                for k, _ in lane_tiles(lanes)
            ],
            axis=1,
        ).astype(jnp.bfloat16)
        out[s] = lax.dot_general(
            total, table_ref[...], (((0,), (0,)), ((), ())), preferred_element_type=jnp.float32
        ).astype(jnp.bfloat16)
        return carry

    lax.fori_loop(0, sources, transform, 0, unroll=8)


def inverse_transform(spectra, table, first, rows, shape, previous):
    owners, width, total, receivers = spectra[0].shape
    length = shape[2]
    lanes = min(LANES, receivers)
    count = len(spectra)
    spec = pl.BlockSpec((owners, width, rows, lanes), lambda i, j: (0, 0, i, j))
    ordered = table.reshape(owners, count, width, length).transpose(1, 0, 2, 3).reshape(length, length)

    def kernel(*refs):
        inverse_kernel(count, *refs)

    in_specs = [spec] * count + [pl.BlockSpec((length, length), lambda i, j: (0, 0))]
    operands = list(spectra) + [ordered]
    aliases = {}
    if previous is not None:
        in_specs.append(pl.BlockSpec(memory_space=pl.ANY))
        operands.append(previous)
        aliases = {count + 1: 0}
    return pl.pallas_call(
        kernel,
        grid=(total // rows, receivers // lanes),
        in_specs=in_specs,
        out_specs=pl.BlockSpec((rows, lanes, length), lambda i, j: (i + first, j, 0)),
        out_shape=jax.ShapeDtypeStruct(shape, jnp.bfloat16),
        scratch_shapes=[pltpu.VMEM((lanes // TILE, length * rows, TILE), jnp.float32)],
        input_output_aliases=aliases,
        compiler_params=pltpu.CompilerParams(vmem_limit_bytes=VMEM),
        name="inverse",
    )(*operands)


def exchange(array):
    return lax.all_to_all(array, OWNERS, 0, 0)


def body(traces):
    sources, _, length = traces.shape
    bands, halves = lax.axis_size("band"), lax.axis_size("rcv")
    owners = bands * halves
    factor = 1.0 / math.sqrt(sources * bands)
    table, inverse = constant_tables(length)
    rest_count = sources - SLAB
    (slab,) = dft(traces, table, rest_count // SLAB, 1, SLAB, owners, 1)
    slab = exchange(slab)
    rest = []
    for part in np.split(table.reshape(owners, -1, length), CHUNKS, axis=1):
        part = part.reshape(length // CHUNKS, length)
        rest += dft(traces, part, 0, rest_count // BLOCK, BLOCK, owners, 1)
    rest = [exchange(part) for part in rest]
    slab_parts, rest_parts = [], []
    for chunk in range(CHUNKS):
        slab_part, rest_part = square(slab, rest[chunk], chunk, bands, halves, factor)
        slab_parts.append(slab_part)
        rest_parts.append(exchange(rest_part))
    last = exchange(jnp.concatenate(slab_parts, axis=1))
    result = inverse_transform(rest_parts, inverse, 0, BLOCK, traces.shape, None)
    return inverse_transform([last], inverse, rest_count // SLAB, SLAB, traces.shape, result)


def complex_right(rows_part):
    real_part = rows_part[:, 0]
    imag_part = rows_part[:, 1]
    first_row = jnp.stack([real_part, imag_part], axis=1)
    second_row = jnp.stack([-imag_part, real_part], axis=1)
    return jnp.stack([first_row, second_row], axis=1)


def complex_product(left_part, rows_part):
    return jnp.einsum(
        "fqsk,fqpkr->fpsr", left_part, complex_right(rows_part), preferred_element_type=jnp.float32
    )


def general_body(traces):
    length = traces.shape[2]
    stations = traces.shape[0] * lax.axis_size("band")
    factor = jnp.float32(1.0 / math.sqrt(stations))
    forward, inverse = tables(length)
    spectra = jnp.einsum("srt,tc->csr", traces, forward, preferred_element_type=jnp.float32).astype(
        jnp.bfloat16
    )
    owned_spec = lax.all_to_all(spectra, "band", split_axis=0, concat_axis=1, tiled=True)
    channels = owned_spec.shape[0]
    owned_spec = owned_spec.reshape(channels // 2, 2, owned_spec.shape[1], owned_spec.shape[2])
    receiver_panel = lax.all_to_all(owned_spec, "rcv", split_axis=2, concat_axis=3, tiled=True)
    block_terms = complex_product(owned_spec, receiver_panel) * factor
    summed = lax.psum_scatter(
        block_terms.astype(jnp.bfloat16), "rcv", scatter_dimension=3, tiled=True
    )
    source_spec = lax.all_to_all(summed, "band", split_axis=2, concat_axis=0, tiled=True)
    result = jnp.einsum("fpsr,fpt->srt", source_spec, inverse, preferred_element_type=jnp.float32)
    return result.astype(jnp.bfloat16)


def choose(traces):
    sources, _, length = traces.shape
    owners = lax.axis_size("band") * lax.axis_size("rcv")
    rest = sources - SLAB
    fits = sources % SLAB == 0 and rest > 0 and rest % BLOCK == 0
    if fits and (length // 2) % (owners * CHUNKS) == 0:
        return body(traces)
    return general_body(traces)


def solution(mesh):
    placed = (P(("grp", "band"), "rcv", None),)
    return jax.shard_map(
        choose, mesh=mesh, in_specs=placed, out_specs=P(("grp", "band"), "rcv", None), check_vma=False
    )
```

```python
import math

import jax
import jax.numpy as jnp
import numpy as np
from jax import lax
from jax.experimental import pallas as pl
from jax.experimental.pallas import tpu as pltpu
from jax.sharding import PartitionSpec as P

OWNERS = ("band", "rcv")
SLAB = 8
BLOCK = 24
CHUNKS = 2
LANES = 256
TILE = 128
VMEM = 62 * 2**20


def tables(length):
    times_int = jnp.arange(length, dtype=jnp.int32)
    freqs_int = jnp.arange(length // 2, dtype=jnp.int32)
    phase_int = times_int[:, None] * freqs_int[None, :] % length
    angles = phase_int.astype(jnp.float32) * jnp.float32(2.0 * math.pi / length)
    factor = jnp.float32(1.0 / math.sqrt(length))
    cosine = jnp.cos(angles) * factor
    sine_part = jnp.sin(angles) * factor
    forward = jnp.stack([cosine, -sine_part], axis=2).reshape(length, length).astype(jnp.bfloat16)
    weights = jnp.where(freqs_int == 0, 1.0, 2.0).astype(jnp.float32)
    inverse = jnp.stack(
        [cosine.T * weights[:, None], -sine_part.T * weights[:, None]], axis=1
    ).astype(jnp.bfloat16)
    return (forward, inverse)


def constant_tables(length):
    phase = np.arange(length // 2)[:, None] * np.arange(length)[None, :] % length
    angles = phase.astype(np.float32) * np.float32(2.0 * math.pi / length)
    factor = np.float32(1.0 / math.sqrt(length))
    forward = np.stack([np.cos(angles) * factor, -(np.sin(angles) * factor)], axis=1)
    weights = np.where(np.arange(length // 2) == 0, 1.0, 2.0).astype(np.float32)
    inverse = forward * weights[:, None, None]
    return [array.reshape(length, length).astype(jnp.bfloat16) for array in (forward, inverse)]


def lane_tiles(lanes):
    return [(k, slice(k * TILE, (k + 1) * TILE)) for k in range(lanes // TILE)]


def dft_kernel(traces_ref, table_ref, *refs):
    outs, scratch = refs[:-1], refs[-1]
    sources = traces_ref.shape[0]
    channels = table_ref.shape[0]
    owners, width = outs[0].shape[0], outs[0].shape[1]

    def transform(s, carry):
        spectrum = lax.dot_general(
            table_ref[...], traces_ref[s], (((1,), (1,)), ((), ())), preferred_element_type=jnp.float32
        )
        for k, lanes in lane_tiles(spectrum.shape[1]):
            scratch[k, pl.ds(s, channels, stride=sources), :] = spectrum[:, lanes]
        return carry

    lax.fori_loop(0, sources, transform, 0, unroll=8)

    def regroup(owner, carry):
        for j, out in enumerate(outs):
            for c in range(width):
                row = (owner * (width * len(outs)) + j * width + c) * sources
                for k, lanes in lane_tiles(out.shape[3]):
                    out[owner, c, :, lanes] = scratch[k, pl.ds(row, sources), :].astype(jnp.bfloat16)
        return carry

    lax.fori_loop(0, owners, regroup, 0, unroll=16)


def dft(traces, table, first, count, rows, owners, chunks):
    _, receivers, length = traces.shape
    lanes = min(LANES, receivers)
    channels = table.shape[0]
    width = channels // (owners * chunks)
    out = jax.ShapeDtypeStruct((owners, width, count * rows, receivers), jnp.bfloat16)
    out_spec = pl.BlockSpec((owners, width, rows, lanes), lambda i, j: (0, 0, i, j))
    return pl.pallas_call(
        dft_kernel,
        grid=(count, receivers // lanes),
        in_specs=[
            pl.BlockSpec((rows, lanes, length), lambda i, j: (i + first, j, 0)),
            pl.BlockSpec((channels, length), lambda i, j: (0, 0)),
        ],
        out_specs=[out_spec] * chunks,
        out_shape=[out] * chunks,
        scratch_shapes=[pltpu.VMEM((lanes // TILE, channels * rows, TILE), jnp.float32)],
        compiler_params=pltpu.CompilerParams(vmem_limit_bytes=VMEM),
        name="dft",
    )(traces, table)


def square_kernel(bands, halves, factor, slab_ref, rest_ref, slab_out, rest_out, real, imag):
    rest = rest_ref.shape[2]
    sources = SLAB + rest
    receivers = rest_ref.shape[3]
    for part, whole in enumerate((real, imag)):
        for b in range(bands):
            for v in range(halves):
                columns = slice(v * receivers, (v + 1) * receivers)
                whole[b * sources : b * sources + rest, columns] = rest_ref[b * halves + v, part]
                whole[b * sources + rest : (b + 1) * sources, columns] = slab_ref[b * halves + v, part]

    def rows(b, carry):
        window = pl.ds(pl.multiple_of(b * sources, sources), sources)
        left_real, left_imag = real[window, :], imag[window, :]
        for v in range(halves):
            columns = slice(v * receivers, (v + 1) * receivers)
            dot = lambda x, y: jnp.dot(x, y[:, columns], preferred_element_type=jnp.float32)
            out_real = (dot(left_real, real) - dot(left_imag, imag)) * factor
            out_imag = (dot(left_real, imag) + dot(left_imag, real)) * factor
            for part, value in enumerate((out_real, out_imag)):
                value = value.astype(jnp.bfloat16)
                rest_out[b * halves + v, part] = value[:rest]
                slab_out[b * halves + v, part] = value[rest:]
        return carry

    lax.fori_loop(0, bands, rows, 0)


def square(slab, rest, chunk, bands, halves, factor):
    owners, width, count, receivers = rest.shape
    freqs = width // 2
    stations = bands * (SLAB + count)
    first = chunk * freqs

    def kernel(*refs):
        square_kernel(bands, halves, factor, *refs)

    slab_spec = pl.BlockSpec((owners, 2, SLAB, receivers), lambda f: (0, f, 0, 0))
    rest_spec = pl.BlockSpec((owners, 2, count, receivers), lambda f: (0, f, 0, 0))
    return pl.pallas_call(
        kernel,
        grid=(freqs,),
        in_specs=[
            pl.BlockSpec((owners, 2, SLAB, receivers), lambda f: (0, f + first, 0, 0)),
            rest_spec,
        ],
        out_specs=[slab_spec, rest_spec],
        out_shape=[
            jax.ShapeDtypeStruct((owners, width, SLAB, receivers), jnp.bfloat16),
            jax.ShapeDtypeStruct(rest.shape, jnp.bfloat16),
        ],
        scratch_shapes=[pltpu.VMEM((stations, stations), jnp.bfloat16)] * 2,
        compiler_params=pltpu.CompilerParams(vmem_limit_bytes=VMEM),
        name="square",
    )(slab, rest)


def inverse_kernel(count, *refs):
    spectra, table_ref = refs[:count], refs[count]
    out, scratch = refs[-2], refs[-1]
    owners, width, sources, lanes = spectra[0].shape
    channels = owners * width
    for j, part in enumerate(spectra):

        def widen(owner, carry):
            for c in range(width):
                row = ((j * owners + owner) * width + c) * sources
                block = part[owner, c].astype(jnp.float32)
                for k, window in lane_tiles(lanes):
                    scratch[k, pl.ds(row, sources), :] = block[:, window]
            return carry

        lax.fori_loop(0, owners, widen, 0, unroll=4)

    def transform(s, carry):
        total = jnp.concatenate(
            [
                scratch[k, pl.ds(s, count * channels, stride=sources), :]
                for k, _ in lane_tiles(lanes)
            ],
            axis=1,
        ).astype(jnp.bfloat16)
        out[s] = lax.dot_general(
            total, table_ref[...], (((0,), (0,)), ((), ())), preferred_element_type=jnp.float32
        ).astype(jnp.bfloat16)
        return carry

    lax.fori_loop(0, sources, transform, 0, unroll=8)


def inverse_transform(spectra, table, first, rows, shape, previous):
    owners, width, total, receivers = spectra[0].shape
    length = shape[2]
    lanes = min(LANES, receivers)
    count = len(spectra)
    spec = pl.BlockSpec((owners, width, rows, lanes), lambda i, j: (0, 0, i, j))
    ordered = table.reshape(owners, count, width, length).transpose(1, 0, 2, 3).reshape(length, length)

    def kernel(*refs):
        inverse_kernel(count, *refs)

    in_specs = [spec] * count + [pl.BlockSpec((length, length), lambda i, j: (0, 0))]
    operands = list(spectra) + [ordered]
    aliases = {}
    if previous is not None:
        in_specs.append(pl.BlockSpec(memory_space=pl.ANY))
        operands.append(previous)
        aliases = {count + 1: 0}
    return pl.pallas_call(
        kernel,
        grid=(total // rows, receivers // lanes),
        in_specs=in_specs,
        out_specs=pl.BlockSpec((rows, lanes, length), lambda i, j: (i + first, j, 0)),
        out_shape=jax.ShapeDtypeStruct(shape, jnp.bfloat16),
        scratch_shapes=[pltpu.VMEM((lanes // TILE, length * rows, TILE), jnp.float32)],
        input_output_aliases=aliases,
        compiler_params=pltpu.CompilerParams(vmem_limit_bytes=VMEM),
        name="inverse",
    )(*operands)


def exchange(array):
    return lax.all_to_all(array, OWNERS, 0, 0)


def body(traces):
    sources, _, length = traces.shape
    bands, halves = lax.axis_size("band"), lax.axis_size("rcv")
    owners = bands * halves
    factor = 1.0 / math.sqrt(sources * bands)
    table, inverse = constant_tables(length)
    rest_count = sources - SLAB
    (slab,) = dft(traces, table, rest_count // SLAB, 1, SLAB, owners, 1)
    slab = exchange(slab)
    rest = []
    for part in np.split(table.reshape(owners, -1, length), CHUNKS, axis=1):
        part = part.reshape(length // CHUNKS, length)
        rest += dft(traces, part, 0, rest_count // BLOCK, BLOCK, owners, 1)
    rest = [exchange(part) for part in rest]
    slab_parts, rest_parts = [], []
    for chunk in range(CHUNKS):
        slab_part, rest_part = square(slab, rest[chunk], chunk, bands, halves, factor)
        slab_parts.append(slab_part)
        rest_parts.append(exchange(rest_part))
    last = exchange(jnp.concatenate(slab_parts, axis=1))
    result = inverse_transform(rest_parts, inverse, 0, BLOCK, traces.shape, None)
    return inverse_transform([last], inverse, rest_count // SLAB, SLAB, traces.shape, result)


def complex_right(rows_part):
    real_part = rows_part[:, 0]
    imag_part = rows_part[:, 1]
    first_row = jnp.stack([real_part, imag_part], axis=1)
    second_row = jnp.stack([-imag_part, real_part], axis=1)
    return jnp.stack([first_row, second_row], axis=1)


def complex_product(left_part, rows_part):
    return jnp.einsum(
        "fqsk,fqpkr->fpsr", left_part, complex_right(rows_part), preferred_element_type=jnp.float32
    )


def general_body(traces):
    length = traces.shape[2]
    stations = traces.shape[0] * lax.axis_size("band")
    factor = jnp.float32(1.0 / math.sqrt(stations))
    forward, inverse = tables(length)
    spectra = jnp.einsum("srt,tc->csr", traces, forward, preferred_element_type=jnp.float32).astype(
        jnp.bfloat16
    )
    owned_spec = lax.all_to_all(spectra, "band", split_axis=0, concat_axis=1, tiled=True)
    channels = owned_spec.shape[0]
    owned_spec = owned_spec.reshape(channels // 2, 2, owned_spec.shape[1], owned_spec.shape[2])
    receiver_panel = lax.all_to_all(owned_spec, "rcv", split_axis=2, concat_axis=3, tiled=True)
    block_terms = complex_product(owned_spec, receiver_panel) * factor
    summed = lax.psum_scatter(
        block_terms.astype(jnp.bfloat16), "rcv", scatter_dimension=3, tiled=True
    )
    source_spec = lax.all_to_all(summed, "band", split_axis=2, concat_axis=0, tiled=True)
    result = jnp.einsum("fpsr,fpt->srt", source_spec, inverse, preferred_element_type=jnp.float32)
    return result.astype(jnp.bfloat16)


def choose(traces):
    sources, _, length = traces.shape
    owners = lax.axis_size("band") * lax.axis_size("rcv")
    rest = sources - SLAB
    fits = sources % SLAB == 0 and rest > 0 and rest % BLOCK == 0
    if fits and (length // 2) % (owners * CHUNKS) == 0:
        return body(traces)
    return general_body(traces)


def solution(mesh):
    placed = (P(("grp", "band"), "rcv", None),)
    return jax.shard_map(
        choose, mesh=mesh, in_specs=placed, out_specs=P(("grp", "band"), "rcv", None), check_vma=False
    )
```
